32 devices in a mesh: groups: 2 (over y), tensor: 4 (over z), rows: 2 (over x), role: 2 (over core).
Axes of the slice: x: 2, y: 2, z: 4, core: 2. Of those that a mesh axis runs over, the one named last changes fastest.
Arguments:
- residual: bfloat16 [64, 8192], P(('groups', 'tensor'), ('rows', 'role')), parts along dimension 0, may hold values from -6 to 6
- attn_gain: float32 [8192], P(('rows', 'role')), may hold values from 0.1 to 1.9
- attn_proj: bfloat16 [3, 8192, 8192], P(None, ('rows', 'role'), 'tensor'), may hold values from -0.0625 to 0.0625
- cache_keys: bfloat16 [64, 32, 8192], P(('groups', 'rows', 'role'), None, 'tensor'), parts along dimension 0, may hold values from -600 to 600
- cache_values: bfloat16 [64, 32, 8192], P(('groups', 'rows', 'role'), None, 'tensor'), parts along dimension 0, may hold values from -6 to 6
- lengths: int32 [64], P(('groups', 'rows', 'role')), parts along dimension 0, may hold values from 1 to 32
- placement: int32 [64], P('groups'), parts along dimension 0, may hold values from 0 to 31, each once
- out_proj: bfloat16 [8192, 8192], P('tensor', ('rows', 'role')), may hold values from -0.0625 to 0.0625
- mix_gain: float32 [8192], P(('rows', 'role')), may hold values from 0.1 to 1.9
- mix_proj: bfloat16 [3, 8192, 8192], P(None, ('rows', 'role'), 'tensor'), may hold values from -0.0625 to 0.0625
- outer_taps: float32 [3, 3, 8192], P(None, None, 'tensor'), may hold values from -1 to 1
- outer_state: bfloat16 [2, 3, 64, 8192], P(None, None, ('groups', 'rows', 'role'), 'tensor'), parts along dimension 2, may hold values from -6 to 6
- inner_taps: float32 [3, 8192], P(None, 'tensor'), may hold values from -1 to 1
- inner_state: bfloat16 [2, 64, 8192], P(None, ('groups', 'rows', 'role'), 'tensor'), parts along dimension 1, may hold values from -6 to 6
Outputs:
- attended: bfloat16 [64, 8192], P(('groups', 'tensor'), ('rows', 'role')), parts along dimension 0
- gated: bfloat16 [64, 8192], P(('groups', 'rows', 'role'), 'tensor'), parts along dimension 0
The draws below stay inside these ranges and needn't reach their ends.
There are 2 independent parts, one for each index of `groups`. The reference program is written for one: setup_inputs(seed, part) draws one part's arguments, and reference() takes and returns one part's arrays. A program takes and returns all parts, laid end to end along the dimension named above; an argument that names none is the same for every part. Nothing has to cross between parts.
Inputs may be any that keep to these rules, and one draw needn't show every extreme that they name: Cache slot s holds lengths[s] cached positions, the first of its 32. `placement`: each row has its own cache slot.
All inputs are finite; a program needn't handle non-finite values.
Results may differ from the reference program's by a relative error of at most 0.017.
Values may be sent and summed in bfloat16 or wider, within the bound.
No kernel may reach another device: no remote copies, remote signals or barrier semaphores. Data moves between devices by JAX's collectives and lax.ppermute only.
A program may use at most 128 MiB of HBM per device.

```python
import math
import jax
import jax.numpy as jnp
from jax import lax

D = 8192
HEADS = 64
HEAD_DIM = 128
CTX = 32
BATCH = 32


def draw_cache_keys(key, part):
    base = jnp.clip(jax.random.normal(jax.random.fold_in(key, 11), (BATCH, CTX, D), jnp.float32), -4.0, 4.0)
    return base.astype(jnp.bfloat16)


def set_ends(drawn, rng, smallest, largest):
    spot = [jax.random.randint(jax.random.fold_in(rng, axis), (), 0, length) for axis, length in enumerate(drawn.shape)]
    longest = drawn.shape.index(max(drawn.shape))
    next_to = spot[:longest] + [(spot[longest] + 1) % drawn.shape[longest]] + spot[longest + 1:]
    return drawn.at[tuple(spot)].set(smallest).at[tuple(next_to)].set(largest)


def shard_levels(stream_key, shape, pieces, low, largest):
    factor_of = 1.0
    for axis_at, blocks in pieces:
        heights = jax.random.uniform(jax.random.fold_in(jax.random.fold_in(stream_key, 6), axis_at), (blocks,), jnp.float32, low / len(pieces), largest / len(pieces))
        factor_of = factor_of * jnp.repeat(jnp.exp(heights), shape[axis_at] // blocks).reshape((-1,) + (1,) * (len(shape) - 1 - axis_at))
    return factor_of


def scatter_about(stream_key, extent, deviation, reach, pieces=(), held_as=jnp.bfloat16):
    entries = deviation * jax.random.normal(stream_key, extent, jnp.float32)
    if pieces:
        entries = entries * shard_levels(stream_key, extent, pieces, -0.22, 0.18)
    return jnp.clip(entries, -reach, reach).astype(held_as)


def setup_inputs(seed: int = 0, part: int = 0) -> dict:
    splits = jax.random.split(jax.random.key(seed), 15)
    part_keys = jax.random.split(jax.random.fold_in(splits[14], part), 15)
    return {
        "residual": scatter_about(part_keys[0], (BATCH, D), 1.0, 6.0, ((0, 4), (1, 4))),
        "attn_gain": jnp.clip(1.0 + 0.18 * jax.random.normal(splits[1], (D,), jnp.float32), 0.1, 1.9),
        "attn_proj": scatter_about(splits[2], (3, D, D), D ** -0.5, 0.0625, ((1, 4), (2, 4))),
        "cache_keys": draw_cache_keys(jax.random.fold_in(jax.random.fold_in(splits[14], part), 71), part),
        "cache_values": scatter_about(part_keys[4], (BATCH, CTX, D), 1.0, 6.0, ((0, 4), (2, 4))),
        "lengths": set_ends(jax.random.randint(part_keys[5], (BATCH,), 1, CTX + 1), jax.random.fold_in(part_keys[5], 1), 1, CTX).astype(jnp.int32),
        "placement": jax.random.permutation(part_keys[6], BATCH).astype(jnp.int32),
        "out_proj": scatter_about(splits[7], (D, D), D ** -0.5, 0.0625, ((0, 4), (1, 4))),
        "mix_gain": jnp.clip(1.0 + 0.18 * jax.random.normal(splits[8], (D,), jnp.float32), 0.1, 1.9),
        "mix_proj": scatter_about(splits[9], (3, D, D), D ** -0.5, 0.0625, ((1, 4), (2, 4))),
        "outer_taps": jnp.clip(jax.random.uniform(splits[10], (3, 3, D), jnp.float32, -1.0, 1.0) * shard_levels(splits[10], (3, 3, D), ((2, 4),), -0.4, 0.0), -1.0, 1.0),
        "outer_state": scatter_about(part_keys[11], (2, 3, BATCH, D), 1.0, 6.0, ((2, 4), (3, 4))),
        "inner_taps": jnp.clip(jax.random.uniform(splits[12], (3, D), jnp.float32, -1.0, 1.0) * shard_levels(splits[12], (3, D), ((1, 4),), -0.4, 0.0), -1.0, 1.0),
        "inner_state": scatter_about(part_keys[13], (2, BATCH, D), 1.0, 6.0, ((1, 4), (2, 4))),
    }


def reference(residual, attn_gain, attn_proj, cache_keys, cache_values, lengths, placement, out_proj, mix_gain, mix_proj, outer_taps, outer_state, inner_taps, inner_state):
    widened = residual.astype(jnp.float32)
    normed = (widened * lax.rsqrt(lax.optimization_barrier(jnp.mean(widened * widened, axis=1, keepdims=True)) + 1e-05) * attn_gain).astype(jnp.bfloat16)
    triple = jnp.stack([jnp.dot(normed, attn_proj[j], preferred_element_type=jnp.float32) for j in range(3)]).astype(jnp.bfloat16)
    inverse = jnp.zeros((BATCH,), jnp.int32).at[placement].set(jnp.arange(BATCH, dtype=jnp.int32))
    ordered = jnp.take(triple, inverse, axis=1)
    query = ordered[0].astype(jnp.float32).reshape(BATCH, HEADS, HEAD_DIM)
    fresh_key = ordered[1].astype(jnp.float32).reshape(BATCH, HEADS, HEAD_DIM)
    fresh_value = ordered[2].astype(jnp.float32).reshape(BATCH, HEADS, HEAD_DIM)
    keys_wide = cache_keys.astype(jnp.float32).reshape(BATCH, CTX, HEADS, HEAD_DIM)
    values_wide = cache_values.astype(jnp.float32).reshape(BATCH, CTX, HEADS, HEAD_DIM)
    scale = 1.0 / math.sqrt(HEAD_DIM)
    scores = jnp.einsum('shd,sphd->shp', query, keys_wide) * scale
    own_score = lax.optimization_barrier(jnp.sum(query * fresh_key, axis=2)) * scale
    live = jnp.arange(CTX, dtype=jnp.int32)[None, None, :] < lengths[:, None, None]
    top_score = jnp.maximum(lax.optimization_barrier(jnp.max(jnp.where(live, scores, -jnp.inf), axis=2)), own_score)
    probs = jnp.where(live, jnp.exp(scores - top_score[:, :, None]), 0.0)
    self_prob = jnp.exp(own_score - top_score)
    total = lax.optimization_barrier(jnp.sum(probs, axis=2)) + self_prob
    weights = (probs / total[:, :, None]).astype(jnp.bfloat16).astype(jnp.float32)
    self_weight = (self_prob / total).astype(jnp.bfloat16).astype(jnp.float32)
    mixed = jnp.einsum('shp,sphd->shd', weights, values_wide) + self_weight[:, :, None] * fresh_value
    slot_out = mixed.reshape(BATCH, D).astype(jnp.bfloat16)
    heads_out = jnp.take(slot_out, placement, axis=0)
    attended = (widened + jnp.dot(heads_out, out_proj, preferred_element_type=jnp.float32)).astype(jnp.bfloat16)
    attended_wide = attended.astype(jnp.float32)
    mix_normed = (attended_wide * lax.rsqrt(lax.optimization_barrier(jnp.mean(attended_wide * attended_wide, axis=1, keepdims=True)) + 1e-05) * mix_gain).astype(jnp.bfloat16)
    branches = jnp.stack([jnp.dot(mix_normed, mix_proj[j], preferred_element_type=jnp.float32) for j in range(3)])
    conv = outer_taps[0][:, None, :] * branches + outer_taps[1][:, None, :] * outer_state[0].astype(jnp.float32) + outer_taps[2][:, None, :] * outer_state[1].astype(jnp.float32)
    product = conv[0] * conv[2]
    filtered = inner_taps[0] * product + inner_taps[1] * inner_state[0].astype(jnp.float32) + inner_taps[2] * inner_state[1].astype(jnp.float32)
    gated = (conv[1] * filtered).astype(jnp.bfloat16)
    return (attended, gated)
```

```python
import functools
import math

import jax
import jax.numpy as jnp
from jax import lax
from jax.experimental import pallas as pl
from jax.experimental.pallas import tpu as pltpu
from jax.sharding import PartitionSpec as P

HEAD_DIM = 128
LANES = 128
EPS = 1e-05
VMEM = pl.BlockSpec(memory_space=pltpu.VMEM)
SMEM = pl.BlockSpec(memory_space=pltpu.SMEM)
ANY = pl.BlockSpec(memory_space=pl.ANY)
F32 = jnp.float32
BF16 = jnp.bfloat16
MIB = 2**20


def shape(dims, dtype):
    return jax.ShapeDtypeStruct(dims, dtype)


def call(kernel, outs, in_specs, scratch=(), limit=12, flops=0, moved=0, out_specs=None):
    return pl.pallas_call(
        kernel,
        out_shape=outs,
        in_specs=in_specs,
        out_specs=out_specs or [VMEM] * len(outs),
        scratch_shapes=scratch,
        compiler_params=pltpu.CompilerParams(vmem_limit_bytes=limit * MIB),
        cost_estimate=pl.CostEstimate(flops=flops, bytes_accessed=moved, transcendentals=0),
    )


def load_kernel(count, *refs):
    sources, _, targets, sems = refs[:count], refs[count], refs[count + 1 : 2 * count + 1], refs[-1]
    copies = [pltpu.make_async_copy(s, t, sems.at[i]) for i, (s, t) in enumerate(zip(sources, targets))]
    for copy in copies:
        copy.start()
    for copy in copies:
        copy.wait()


def load(arrays, after):
    moved = sum(a.size * a.dtype.itemsize for a in arrays)
    return call(
        functools.partial(load_kernel, len(arrays)),
        [pltpu.VMEM(a.shape, a.dtype) for a in arrays],
        [ANY] * (len(arrays) + 1),
        scratch=[pltpu.SemaphoreType.DMA((len(arrays),))],
        limit=2,
        flops=moved * 100,
        moved=moved,
    )(*[pltpu.with_memory_space_constraint(a, pltpu.HBM) for a in arrays], after)


def project(xp, gain, w_ref, own_ref, sends):
    block = own_ref.shape[0]
    width = w_ref.shape[2]
    squares = jnp.sum(xp * xp, axis=1, keepdims=True)
    gained = (xp * gain).astype(BF16)
    chunk = min(512, width)
    for j in range(3):
        for c in range(0, width, chunk):
            out = jnp.dot(gained, w_ref[j, :, c : c + chunk], preferred_element_type=F32)
            at = j * width + c
            own_ref[:, at : at + chunk] = out[:block]
            for e, send in enumerate(sends, 1):
                send[:, at : at + chunk] = out[e * block : (e + 1) * block].astype(BF16)
    lane = lax.broadcasted_iota(jnp.int32, (xp.shape[0], LANES), 1)
    high = squares.astype(BF16).astype(F32)
    rest = squares - high
    middle = rest.astype(BF16).astype(F32)
    low = rest - middle
    tail = jnp.where(lane == 0, high, jnp.where(lane == 1, middle, jnp.where(lane == 2, low, 0.0)))
    own_ref[:, 3 * width :] = tail[:block]
    for e, send in enumerate(sends, 1):
        send[:, 3 * width :] = tail[e * block : (e + 1) * block].astype(BF16)


def collect(features, own_ref, received):
    width = (own_ref.shape[1] - LANES) // 3
    total = own_ref[...]
    for ref in received:
        total = total + ref[...].astype(F32)
    squares = jnp.sum(total[:, 3 * width :], axis=1, keepdims=True)
    scale = lax.rsqrt(squares / features + EPS)
    return [total[:, j * width : (j + 1) * width] * scale for j in range(3)]


def first_kernel(n_t, n_g, *refs):
    parts, (index_ref, onehot_ref, gain_ref, w_ref) = refs[:n_t], refs[n_t : n_t + 4]
    x_ref, own_ref, *sends = refs[n_t + 4 :]
    rows = parts[0].shape[0]
    t = index_ref[0]
    for d in range(n_t):
        at = pl.multiple_of((t ^ d) * rows, rows)
        x_ref[pl.ds(at, rows), :] = parts[d][...].astype(F32)
    xp = jnp.dot(onehot_ref[...], x_ref[...].astype(BF16), preferred_element_type=F32)
    project(xp, gain_ref[...], w_ref, own_ref, sends)


def attend_kernel(n_g, features, *refs):
    own_ref, received = refs[0], refs[1:n_g]
    lengths_ref, keys_ref, values_ref, out_ref, rows_ref = refs[n_g:]
    slots, positions, width = keys_ref.shape
    heads = width // HEAD_DIM
    query, fresh_key, fresh_value = [
        a.astype(BF16).astype(F32) for a in collect(features, own_ref, received)
    ]
    mine = (
        lax.broadcasted_iota(jnp.int32, (heads, width), 1) // HEAD_DIM
        == lax.broadcasted_iota(jnp.int32, (heads, width), 0)
    )
    scale = 1.0 / math.sqrt(HEAD_DIM)
    position = lax.broadcasted_iota(jnp.int32, (heads, positions), 1)
    for s in range(slots):
        spread = jnp.where(mine, query[s : s + 1], 0.0)
        scores = scale * lax.dot_general(
            spread.astype(BF16), keys_ref[s], (((1,), (1,)), ((), ())), preferred_element_type=F32
        )
        own_score = scale * jnp.sum(spread * fresh_key[s : s + 1], axis=1, keepdims=True)
        live = position < lengths_ref[s]
        top = jnp.maximum(
            jnp.max(jnp.where(live, scores, -jnp.inf), axis=1, keepdims=True), own_score
        )
        probs = jnp.where(live, jnp.exp(scores - top), 0.0)
        self_prob = jnp.exp(own_score - top)
        total = jnp.sum(probs, axis=1, keepdims=True) + self_prob
        weights = (probs / total).astype(BF16)
        self_weight = (self_prob / total).astype(BF16).astype(F32)
        mixed = jnp.dot(weights, values_ref[s], preferred_element_type=F32)
        mixed = mixed + self_weight * fresh_value[s : s + 1]
        rows_ref[s : s + 1, :] = jnp.sum(jnp.where(mine, mixed, 0.0), axis=0, keepdims=True)
    out_ref[...] = rows_ref[...].astype(BF16)


def out_kernel(n_g, *refs):
    parts, (onehot_ref, w_ref) = refs[:n_g], refs[n_g : n_g + 2]
    own_ref, send_ref = refs[n_g + 2 :]
    gathered = jnp.concatenate([p[...].astype(F32) for p in parts], axis=0).astype(BF16)
    rows = jnp.dot(onehot_ref[...], gathered, preferred_element_type=F32).astype(BF16)
    width = w_ref.shape[1]
    chunk = min(512, width)
    for c in range(0, width, chunk):
        out = jnp.dot(rows, w_ref[:, c : c + chunk], preferred_element_type=F32)
        own_ref[:, c : c + chunk] = out
        send_ref[:, c : c + chunk] = out.astype(BF16)


def second_kernel(n_t, n_g, *refs):
    index_ref, x_ref, terms_ref = refs[:3]
    received = refs[3 : n_t + 2]
    gain_ref, w_ref, attended_ref, own_ref, *sends, scratch = refs[n_t + 2 :]
    rows, block = attended_ref.shape[0], own_ref.shape[0]
    total = terms_ref[...]
    for ref in received:
        total = total + ref[...].astype(F32)
    scratch[...] = (x_ref[...] + total).astype(BF16).astype(F32)
    at = pl.multiple_of(index_ref[0] * rows, rows)
    attended_ref[...] = scratch[pl.ds(at, rows), :].astype(BF16)
    g = index_ref[1]
    xp = jnp.concatenate(
        [scratch[pl.ds(pl.multiple_of((g ^ e) * block, block), block), :] for e in range(n_g)], axis=0
    )
    project(xp, gain_ref[...], w_ref, own_ref, sends)


def mixer_kernel(n_g, features, *refs):
    own_ref, received = refs[0], refs[1:n_g]
    outer_taps, outer_state, inner_taps, inner_state, out_ref = refs[n_g:]
    branches = collect(features, own_ref, received)
    conv = [
        outer_taps[0, j : j + 1] * branches[j]
        + outer_taps[1, j : j + 1] * outer_state[0, j].astype(F32)
        + outer_taps[2, j : j + 1] * outer_state[1, j].astype(F32)
        for j in range(3)
    ]
    filtered = (
        inner_taps[0:1] * (conv[0] * conv[2])
        + inner_taps[1:2] * inner_state[0].astype(F32)
        + inner_taps[2:3] * inner_state[1].astype(F32)
    )
    out_ref[...] = (conv[1] * filtered).astype(BF16)


def local(
    n_t,
    n_g,
    residual,
    attn_gain,
    attn_proj,
    cache_keys,
    cache_values,
    lengths,
    placement,
    out_proj,
    mix_gain,
    mix_proj,
    outer_taps,
    outer_state,
    inner_taps,
    inner_state,
):
    group = ("rows", "role")
    rows, depth = residual.shape
    slots = lengths.shape[0]
    batch = placement.shape[0]
    width = attn_proj.shape[2]
    features = depth * n_g
    t = lax.axis_index("tensor")
    g = lax.axis_index(group)
    index = jnp.stack([t, g]).astype(jnp.int32)

    def swap(x, axes, n, d):
        return lax.ppermute(x, axes, [(i, i ^ d) for i in range(n)])

    def products(n):
        return 2 * batch * depth * n

    parts = [residual] + [swap(residual, "tensor", n_t, d) for d in range(1, n_t)]
    place = jnp.arange(batch, dtype=jnp.int32)
    slot_of = ((g ^ (place // slots)) * slots + place % slots).astype(jnp.int32)
    to_slots = (slot_of[:, None] == placement[None, :]).astype(BF16)
    to_rows = (placement[:, None] == slot_of[None, :]).astype(BF16)

    (attn_w,) = load([attn_proj], index)
    payload = 3 * width + LANES
    branch_outs = [shape((slots, payload), F32)] + [shape((slots, payload), BF16)] * (n_g - 1)
    x, own, *sends = call(
        functools.partial(first_kernel, n_t, n_g),
        [shape((batch, depth), F32)] + branch_outs,
        [VMEM] * n_t + [SMEM] + [VMEM] * 3,
        flops=products(3 * width),
        moved=attn_proj.size * 2,
    )(*parts, index, to_slots, attn_gain.reshape(1, depth), attn_w)

    received = [swap(s, group, n_g, e) for e, s in enumerate(sends, 1)]
    keys, values, out_w = load([cache_keys, cache_values, out_proj], own)
    (slot_out,) = call(
        functools.partial(attend_kernel, n_g, features),
        [shape((slots, width), BF16)],
        [VMEM] * n_g + [SMEM, VMEM, VMEM],
        scratch=[pltpu.VMEM((slots, width), F32)],
        flops=4 * cache_keys.size,
        moved=cache_keys.size * 4,
    )(own, *received, lengths, keys, values)

    gathered = [slot_out] + [swap(slot_out, group, n_g, e) for e in range(1, n_g)]
    terms, send = call(
        functools.partial(out_kernel, n_g),
        [shape((batch, depth), F32), shape((batch, depth), BF16)],
        [VMEM] * (n_g + 2),
        flops=products(depth),
        moved=out_proj.size * 2,
    )(*gathered, to_rows, out_w)

    received = [swap(send, "tensor", n_t, d) for d in range(1, n_t)]
    (mix_w,) = load([mix_proj], terms)
    attended, own, *sends = call(
        functools.partial(second_kernel, n_t, n_g),
        [shape((rows, depth), BF16)] + branch_outs,
        [SMEM] + [VMEM] * (n_t + 3),
        scratch=[pltpu.VMEM((batch, depth), F32)],
        flops=products(3 * width),
        moved=mix_proj.size * 2,
    )(index, x, terms, *received, mix_gain.reshape(1, depth), mix_w)

    received = [swap(s, group, n_g, e) for e, s in enumerate(sends, 1)]
    (gated,) = call(
        functools.partial(mixer_kernel, n_g, features),
        [shape((slots, width), BF16)],
        [VMEM] * (n_g + 4),
        flops=slots * width * 40,
        moved=slots * width * 40,
    )(own, *received, outer_taps, outer_state, inner_taps, inner_state)
    return (attended, gated)


def solution(mesh):
    n_t = mesh.shape["tensor"]
    n_g = mesh.shape["rows"] * mesh.shape["role"]
    for n in (n_t, n_g):
        assert n & (n - 1) == 0, "axis size"
    return jax.shard_map(
        functools.partial(local, n_t, n_g),
        mesh=mesh,
        in_specs=(
            P(("groups", "tensor"), ("rows", "role")),
            P(("rows", "role")),
            P(None, ("rows", "role"), "tensor"),
            P(("groups", "rows", "role"), None, "tensor"),
            P(("groups", "rows", "role"), None, "tensor"),
            P(("groups", "rows", "role")),
            P("groups"),
            P("tensor", ("rows", "role")),
            P(("rows", "role")),
            P(None, ("rows", "role"), "tensor"),
            P(None, None, "tensor"),
            P(None, None, ("groups", "rows", "role"), "tensor"),
            P(None, "tensor"),
            P(None, ("groups", "rows", "role"), "tensor"),
        ),
        out_specs=(
            P(("groups", "tensor"), ("rows", "role")),
            P(("groups", "rows", "role"), "tensor"),
        ),
        check_vma=False,
    )
```

```python
import functools
import math

import jax
import jax.numpy as jnp
from jax import lax
from jax.experimental import pallas as pl
from jax.experimental.pallas import tpu as pltpu
from jax.sharding import PartitionSpec as P

HEAD_DIM = 128
LANES = 128
EPS = 1e-05
GROUP = ("rows", "role")
VMEM = pl.BlockSpec(memory_space=pltpu.VMEM)
SMEM = pl.BlockSpec(memory_space=pltpu.SMEM)
ANY = pl.BlockSpec(memory_space=pl.ANY)
F32 = jnp.float32
BF16 = jnp.bfloat16
MIB = 2**20
FIRST_SPLIT = (3,)
SECOND_SPLIT = (3,)
PIECES = 1


def shape(dims, dtype):
    return jax.ShapeDtypeStruct(dims, dtype)


def call(kernel, outs, in_specs, scratch=(), limit=6, flops=0, moved=0, loads=(), ordered=()):
    n_in, n_out, n_load, n_held = len(in_specs), len(outs), len(loads), len(loads) + len(ordered)

    def body(*refs):
        ins, sources, outs = refs[:n_in], refs[n_in : n_in + n_load], refs[n_in + n_held :]
        targets, rest = outs[n_out : n_out + n_load], outs[n_out + n_load :]
        copies = [
            pltpu.make_async_copy(source.at[window], target, rest[-1].at[i])
            for i, (source, target, (_, window, _)) in enumerate(zip(sources, targets, loads))
        ]
        for copy in copies:
            copy.start()
        kernel(*ins, *outs[:n_out], *rest[: len(scratch)])
        for copy in copies:
            copy.wait()

    function = pl.pallas_call(
        body,
        out_shape=list(outs) + [pltpu.VMEM(dims, a.dtype) for a, _, dims in loads],
        in_specs=list(in_specs) + [ANY] * n_held,
        out_specs=[VMEM] * n_out + [ANY] * n_load,
        scratch_shapes=list(scratch) + ([pltpu.SemaphoreType.DMA((n_load,))] if loads else []),
        compiler_params=pltpu.CompilerParams(vmem_limit_bytes=limit * MIB),
        cost_estimate=pl.CostEstimate(
            flops=flops,
            bytes_accessed=moved + sum(2 * math.prod(dims) for _, _, dims in loads),
            transcendentals=0,
        ),
    )
    held = [pltpu.with_memory_space_constraint(a, pltpu.HBM) for a, _, _ in loads]
    return lambda *operands: function(*operands, *held, *ordered)


def whole(array):
    return array, tuple(slice(None) for _ in array.shape), array.shape


def load_kernel(after_ref):
    pass


def load(loads, after):
    moved = sum(math.prod(dims) for _, _, dims in loads)
    return call(load_kernel, [], [ANY], limit=2, flops=moved * 200, loads=loads)(after)


def chunks(width):
    size = min(512, width)
    return [slice(c, c + size) for c in range(0, width, size)]


def tail_of(squares):
    lane = lax.broadcasted_iota(jnp.int32, (squares.shape[0], LANES), 1)
    high = squares.astype(BF16).astype(F32)
    middle = (squares - high).astype(BF16).astype(F32)
    low = squares - high - middle
    return jnp.where(lane == 0, high, jnp.where(lane == 1, middle, jnp.where(lane == 2, low, 0.0)))


def deliver(value, at, own_ref, sends):
    block = own_ref.shape[0]
    own_ref[:, at] = value[:block]
    for e, send in enumerate(sends, 1):
        send[:, at] = value[e * block : (e + 1) * block].astype(BF16)


def slot_onehot(placement, slots):
    batch = placement.shape[1]
    at = lax.broadcasted_iota(jnp.int32, (batch, batch), 0)
    slot = (lax.axis_index(GROUP) ^ (at // slots)) * slots + at % slots
    return (slot == placement).astype(F32).astype(BF16)


def head_kernel(out_ref):
    out_ref[...] = jnp.zeros_like(out_ref)


def first_kernel(n_t, products, *refs):
    parts, (placement_ref, gain_ref, w_ref) = refs[:n_t], refs[n_t : n_t + 3]
    x_ref, gained_ref, own_ref, *sends = refs[n_t + 3 :]
    rows = parts[0].shape[0]
    t = lax.axis_index("tensor")
    for d in range(n_t):
        at = pl.multiple_of((t ^ d) * rows, rows)
        x_ref[pl.ds(at, rows), :] = parts[d][...].astype(F32)
    onehot = slot_onehot(placement_ref[...], own_ref.shape[0])
    xp = jnp.dot(onehot, x_ref[...].astype(BF16), preferred_element_type=F32)
    gained = (xp * gain_ref[...]).astype(BF16)
    gained_ref[...] = gained
    tail = tail_of(jnp.sum(xp * xp, axis=1, keepdims=True))
    width = w_ref.shape[2]
    deliver(tail, slice(products * width, products * width + LANES), own_ref, sends)
    for j in range(products):
        for c in chunks(width):
            out = jnp.dot(gained, w_ref[j, :, c], preferred_element_type=F32)
            deliver(out, slice(j * width + c.start, j * width + c.stop), own_ref, sends)


def more_kernel(start, products, gained_ref, w_ref, own_ref, *sends):
    width = w_ref.shape[2]
    gained = gained_ref[...]
    for j in range(products):
        for c in chunks(width):
            out = jnp.dot(gained, w_ref[start + j, :, c], preferred_element_type=F32)
            deliver(out, slice(j * width + c.start, j * width + c.stop), own_ref, sends)


def collect(features, width, n_g, counts, refs):
    products = []
    for i, count in enumerate(counts):
        own_ref, *received = refs[i * n_g : (i + 1) * n_g]
        total = own_ref[...]
        for ref in received:
            total = total + ref[...].astype(F32)
        products += [total[:, j * width : (j + 1) * width] for j in range(count)]
        if i == 0:
            squares = jnp.sum(total[:, count * width :], axis=1, keepdims=True)
            scale = lax.rsqrt(squares / features + EPS)
    return [p * scale for p in products]


def attend_kernel(n_g, features, counts, *refs):
    n = n_g * len(counts)
    lengths_ref, keys_ref, values_ref, out_ref = refs[n:]
    slots, width = out_ref.shape
    columns = keys_ref.shape[0]
    positions = columns // slots
    query, fresh_key, fresh_value = [
        p.astype(BF16).astype(F32) for p in collect(features, width, n_g, counts, refs[:n])
    ]
    scale = 1.0 / math.sqrt(HEAD_DIM)
    column = lax.broadcasted_iota(jnp.int32, (slots, columns), 1)
    slot = lax.broadcasted_iota(jnp.int32, (slots, columns), 0)
    length = jnp.zeros((slots, columns), jnp.int32)
    for s in range(slots):
        length = jnp.where(slot == s, lengths_ref[s], length)
    live = (column >= slot * positions) & (column < slot * positions + length)
    heads = [slice(h, h + HEAD_DIM) for h in range(0, width, HEAD_DIM)]
    scores = [
        scale
        * lax.dot_general(
            query[:, h].astype(BF16), keys_ref[:, h], (((1,), (1,)), ((), ())), preferred_element_type=F32
        )
        for h in heads
    ]
    own_scores = [scale * jnp.sum(query[:, h] * fresh_key[:, h], axis=1, keepdims=True) for h in heads]
    mixed = []
    for h, score, own_score in zip(heads, scores, own_scores):
        top = jnp.maximum(jnp.max(jnp.where(live, score, -jnp.inf), axis=1, keepdims=True), own_score)
        probs = jnp.where(live, jnp.exp(score - top), 0.0)
        self_prob = jnp.exp(own_score - top)
        total = jnp.sum(probs, axis=1, keepdims=True) + self_prob
        weights = (probs / total).astype(BF16)
        self_weight = (self_prob / total).astype(BF16).astype(F32)
        out = jnp.dot(weights, values_ref[:, h], preferred_element_type=F32)
        out_ref[:, h] = (out + self_weight * fresh_value[:, h]).astype(BF16)


def out_kernel(n_g, pieces, *refs):
    parts, (placement_ref, w_ref) = refs[:n_g], refs[n_g : n_g + 2]
    owns, sends = refs[n_g + 2 :: 2], refs[n_g + 3 :: 2]
    gathered = jnp.concatenate([p[...].astype(F32) for p in parts], axis=0).astype(BF16)
    onehot = slot_onehot(placement_ref[...], parts[0].shape[0])
    rows = lax.dot_general(
        onehot, gathered, (((0,), (0,)), ((), ())), preferred_element_type=F32
    ).astype(BF16)
    width = w_ref.shape[1] // pieces
    for own_ref, send_ref, start in zip(owns, sends, range(0, w_ref.shape[1], width)):
        for c in chunks(width):
            out = jnp.dot(
                rows, w_ref[:, start + c.start : start + c.stop], preferred_element_type=F32
            )
            own_ref[:, c] = out
            send_ref[:, c] = out.astype(BF16)


def join(n_t, n_g, block, piece, x_ref, terms_ref, received, gain_ref, attended_ref, scratch):
    rows, width = attended_ref.shape
    columns = slice(piece * width, (piece + 1) * width)
    total = terms_ref[...]
    for ref in received:
        total = total + ref[...].astype(F32)
    scratch[...] = (x_ref[:, columns] + total).astype(BF16).astype(F32)
    at = pl.multiple_of(lax.axis_index("tensor") * rows, rows)
    attended_ref[...] = scratch[pl.ds(at, rows), :].astype(BF16)
    g = lax.axis_index(GROUP)
    xp = jnp.concatenate(
        [scratch[pl.ds(pl.multiple_of((g ^ e) * block, block), block), :] for e in range(n_g)], axis=0
    )
    return jnp.sum(xp * xp, axis=1, keepdims=True), (xp * gain_ref[:, columns]).astype(BF16)


def piece_kernel(n_t, n_g, block, piece, *refs):
    x_ref, terms_ref, *received = refs[: n_t + 1]
    gain_ref, w_ref = refs[n_t + 1 : n_t + 3]
    before, (attended_ref, sums_ref, squares_ref, scratch) = refs[n_t + 3 : -4], refs[-4:]
    squares, gained = join(
        n_t, n_g, block, piece, x_ref, terms_ref, received, gain_ref, attended_ref, scratch
    )
    squares_ref[...] = (before[1][...] if before else 0.0) + jnp.broadcast_to(squares, squares_ref.shape)
    width = w_ref.shape[2]
    for j in range(3):
        for c in chunks(width):
            at = slice(j * width + c.start, j * width + c.stop)
            out = jnp.dot(gained, w_ref[j, :, c], preferred_element_type=F32)
            sums_ref[:, at] = out + before[0][:, at] if before else out


def last_kernel(n_t, n_g, piece, products, *refs):
    x_ref, terms_ref, *received = refs[: n_t + 1]
    gain_ref, w_ref = refs[n_t + 1 : n_t + 3]
    before = refs[n_t + 3 : -(n_g + 3)]
    attended_ref, gained_ref, own_ref, *sends, scratch = refs[-(n_g + 3) :]
    squares, gained = join(
        n_t, n_g, own_ref.shape[0], piece, x_ref, terms_ref, received, gain_ref, attended_ref, scratch
    )
    gained_ref[...] = gained
    if before:
        squares = squares + before[1][:, :1]
    width = w_ref.shape[2]
    deliver(
        tail_of(squares), slice(products * width, products * width + LANES), own_ref, sends
    )
    for j in range(products):
        for c in chunks(width):
            at = slice(j * width + c.start, j * width + c.stop)
            out = jnp.dot(gained, w_ref[j, :, c], preferred_element_type=F32)
            deliver(out + before[0][:, at] if before else out, at, own_ref, sends)


def tail_products_kernel(n_g, start, products, *refs):
    gained_ref, w_ref, *before = refs[:-n_g]
    own_ref, *sends = refs[-n_g:]
    width = w_ref.shape[2]
    gained = gained_ref[...]
    for j in range(products):
        for c in chunks(width):
            out = jnp.dot(gained, w_ref[start + j, :, c], preferred_element_type=F32)
            if before:
                at = (start + j) * width
                out = out + before[0][:, at + c.start : at + c.stop]
            deliver(out, slice(j * width + c.start, j * width + c.stop), own_ref, sends)


def mixer_kernel(n_g, features, counts, *refs):
    n = n_g * len(counts)
    outer_taps, outer_state, inner_taps, inner_state, out_ref = refs[n:]
    branches = collect(features, out_ref.shape[1], n_g, counts, refs[:n])
    conv = [
        outer_taps[0, j : j + 1] * branches[j]
        + outer_taps[1, j : j + 1] * outer_state[0, j].astype(F32)
        + outer_taps[2, j : j + 1] * outer_state[1, j].astype(F32)
        for j in range(3)
    ]
    filtered = (
        inner_taps[0:1] * (conv[0] * conv[2])
        + inner_taps[1:2] * inner_state[0].astype(F32)
        + inner_taps[2:3] * inner_state[1].astype(F32)
    )
    out_ref[...] = (conv[1] * filtered).astype(BF16)


def local(
    n_t,
    n_g,
    residual,
    attn_gain,
    attn_proj,
    cache_keys,
    cache_values,
    lengths,
    placement,
    out_proj,
    mix_gain,
    mix_proj,
    outer_taps,
    outer_state,
    inner_taps,
    inner_state,
):
    rows, depth = residual.shape
    slots = lengths.shape[0]
    batch = placement.shape[0]
    width = attn_proj.shape[2]
    features = depth * n_g
    placement = placement.reshape(1, batch)
    attn_gain, mix_gain = attn_gain.reshape(1, depth), mix_gain.reshape(1, depth)

    def swap(x, axes, n):
        return [lax.ppermute(x[d - 1], axes, [(i, i ^ d) for i in range(n)]) for d in range(1, n)]

    def blocks(products, tail):
        columns = products * width + tail
        return [shape((slots, columns), F32)] + [shape((slots, columns), BF16)] * (n_g - 1)

    def cost(k, n):
        return dict(flops=2 * batch * k * n, moved=2 * k * n)

    (head,) = call(head_kernel, [shape((8, LANES), F32)], [], limit=2, flops=attn_proj.size * 64 * 40, moved=attn_proj.size * 80)()
    residual, head = lax.optimization_barrier((residual, head))
    parts = [residual] + swap([residual] * n_t, "tensor", n_t)
    attn_w = pltpu.with_memory_space_constraint(attn_proj, pltpu.VMEM)
    count = FIRST_SPLIT[0]
    keys, values = [c.reshape(-1, width) for c in (cache_keys, cache_values)]
    x, gained, own, *sends, keys, values, out_w = call(
        functools.partial(first_kernel, n_t, count),
        [shape((batch, depth), F32), shape((batch, depth), BF16)] + blocks(count, LANES),
        [VMEM] * (n_t + 3),
        **cost(depth, count * width),
        loads=[whole(keys), whole(values), whole(out_proj)],
        ordered=[head],
    )(*parts, placement, attn_gain, attn_w)
    arrived = [own] + swap(sends, GROUP, n_g)
    start = count
    for count in FIRST_SPLIT[1:]:
        own, *sends = call(
            functools.partial(more_kernel, start, count),
            blocks(count, 0),
            [VMEM] * 2,
            **cost(depth, count * width),
        )(gained, attn_w)
        arrived += [own] + swap(sends, GROUP, n_g)
        start += count

    part = depth // PIECES
    def piece_of(p):
        return mix_proj, (slice(None), slice(p * part, (p + 1) * part), slice(None)), (3, part, width)

    (slot_out,) = call(
        functools.partial(attend_kernel, n_g, features, FIRST_SPLIT),
        [shape((slots, width), BF16)],
        [VMEM] * len(arrived) + [SMEM, VMEM, VMEM],
        flops=4 * cache_keys.size,
        moved=cache_keys.size * 4,
        ordered=(),
    )(*arrived, lengths, keys, values)

    gathered = [slot_out] + swap([slot_out] * n_g, GROUP, n_g)
    terms = call(
        functools.partial(out_kernel, n_g, PIECES),
        [shape((batch, part), F32), shape((batch, part), BF16)] * PIECES,
        [VMEM] * (n_g + 2),
        **cost(width, depth),
        ordered=(),
    )(*gathered, placement, out_w)

    received = [swap([terms[2 * p + 1]] * n_t, "tensor", n_t) for p in range(PIECES)]
    mix_w = load([piece_of(p) for p in range(PIECES)], terms[0])
    attended, before = [], []
    for p in range(PIECES - 1):
        out, *before = call(
            functools.partial(piece_kernel, n_t, n_g, slots, p),
            [shape((rows, part), BF16), shape((batch, 3 * width), F32), shape((batch, LANES), F32)],
            [VMEM] * (n_t + 3 + len(before)),
            scratch=[pltpu.VMEM((batch, part), F32)],
            **cost(part, 3 * width),
        )(x, terms[2 * p], *received[p], mix_gain, mix_w[p], *before)
        attended.append(out)
    count = SECOND_SPLIT[0]
    out, gained, own, *sends = call(
        functools.partial(last_kernel, n_t, n_g, PIECES - 1, count),
        [shape((rows, part), BF16), shape((batch, part), BF16)] + blocks(count, LANES),
        [VMEM] * (n_t + 3 + len(before)),
        scratch=[pltpu.VMEM((batch, part), F32)],
        **cost(part, count * width),
    )(x, terms[-2], *received[-1], mix_gain, mix_w[-1], *before)
    attended.append(out)
    arrived = [own] + swap(sends, GROUP, n_g)
    start = count
    for count in SECOND_SPLIT[1:]:
        own, *sends = call(
            functools.partial(tail_products_kernel, n_g, start, count),
            blocks(count, 0),
            [VMEM] * (2 + len(before[:1])),
            **cost(part, count * width),
        )(gained, mix_w[-1], *before[:1])
        arrived += [own] + swap(sends, GROUP, n_g)
        start += count
    (gated,) = call(
        functools.partial(mixer_kernel, n_g, features, SECOND_SPLIT),
        [shape((slots, width), BF16)],
        [VMEM] * (len(arrived) + 4),
        flops=slots * width * 40,
        moved=slots * width * 40,
    )(*arrived, outer_taps, outer_state, inner_taps, inner_state)
    return (jnp.concatenate(attended, axis=1), gated)


def solution(mesh):
    n_t = mesh.shape["tensor"]
    n_g = mesh.shape["rows"] * mesh.shape["role"]
    for n in (n_t, n_g):
        assert n & (n - 1) == 0, "axis size"
    return jax.shard_map(
        functools.partial(local, n_t, n_g),
        mesh=mesh,
        in_specs=(
            P(("groups", "tensor"), ("rows", "role")),
            P(("rows", "role")),
            P(None, ("rows", "role"), "tensor"),
            P(("groups", "rows", "role"), None, "tensor"),
            P(("groups", "rows", "role"), None, "tensor"),
            P(("groups", "rows", "role")),
            P("groups"),
            P("tensor", ("rows", "role")),
            P(("rows", "role")),
            P(None, ("rows", "role"), "tensor"),
            P(None, None, "tensor"),
            P(None, None, ("groups", "rows", "role"), "tensor"),
            P(None, "tensor"),
            P(None, ("groups", "rows", "role"), "tensor"),
        ),
        out_specs=(
            P(("groups", "tensor"), ("rows", "role")),
            P(("groups", "rows", "role"), "tensor"),
        ),
        check_vma=False,
    )
```

```python
import functools
import math

import jax
import jax.numpy as jnp
from jax import lax
from jax.experimental import pallas as pl
from jax.experimental.pallas import tpu as pltpu
from jax.sharding import PartitionSpec as P


HEAD_DIM = 128
LANES = 128
EPS = 1e-05
GROUP = ("rows", "role")
VMEM = pl.BlockSpec(memory_space=pltpu.VMEM)
SMEM = pl.BlockSpec(memory_space=pltpu.SMEM)
ANY = pl.BlockSpec(memory_space=pl.ANY)
F32 = jnp.float32
BF16 = jnp.bfloat16
MIB = 2**20
FIRST_SPLIT = (2, 1)
SECOND_SPLIT = (1, 2)
PIECES = 2
SHARE = 4


def shape(dims, dtype):
    return jax.ShapeDtypeStruct(dims, dtype)


def call(kernel, outs, in_specs, scratch=(), limit=6, flops=0, moved=0, loads=(), ordered=()):
    n_in, n_out, n_load, n_held = len(in_specs), len(outs), len(loads), len(loads) + len(ordered)

    def body(*refs):
        ins, sources, outs = refs[:n_in], refs[n_in : n_in + n_load], refs[n_in + n_held :]
        targets, rest = outs[n_out : n_out + n_load], outs[n_out + n_load :]
        copies = [
            pltpu.make_async_copy(source.at[window], target, rest[-1].at[i])
            for i, (source, target, (_, window, _)) in enumerate(zip(sources, targets, loads))
        ]
        for copy in copies:
            copy.start()
        kernel(*ins, *outs[:n_out], *rest[: len(scratch)])
        for copy in copies:
            copy.wait()

    function = pl.pallas_call(
        body,
        out_shape=list(outs) + [pltpu.VMEM(dims, a.dtype) for a, _, dims in loads],
        in_specs=list(in_specs) + [ANY] * n_held,
        out_specs=[VMEM] * n_out + [ANY] * n_load,
        scratch_shapes=list(scratch) + ([pltpu.SemaphoreType.DMA((n_load,))] if loads else []),
        compiler_params=pltpu.CompilerParams(vmem_limit_bytes=limit * MIB),
        cost_estimate=pl.CostEstimate(
            flops=flops,
            bytes_accessed=moved,
            transcendentals=0,
        ),
    )
    held = [pltpu.with_memory_space_constraint(a, pltpu.HBM) for a, _, _ in loads]
    return lambda *operands: function(*operands, *held, *ordered)


def whole(array):
    return array, tuple(slice(None) for _ in array.shape), array.shape


def load_kernel(after_ref):
    pass


def load(loads, after):
    return call(load_kernel, [], [ANY], limit=2, loads=loads)(after)


def chunks(width):
    return [slice(c, min(c + 512, width)) for c in range(0, width, 512)]


def tail_of(squares):
    lane = lax.broadcasted_iota(jnp.int32, (squares.shape[0], LANES), 1) - 3 * lax.axis_index("role")
    high = squares.astype(BF16).astype(F32)
    middle = (squares - high).astype(BF16).astype(F32)
    low = squares - high - middle
    return jnp.where(lane == 0, high, jnp.where(lane == 1, middle, jnp.where(lane == 2, low, 0.0)))


def deliver(value, at, own_ref, sends):
    block = own_ref.shape[0]
    own_ref[:, at] = value[:block]
    for e, send in enumerate(sends, 1):
        send[:, at] = value[e * block : (e + 1) * block].astype(send.dtype)


def slot_onehot(placement, slots, n_x):
    batch = placement.shape[1]
    n_r = batch // slots // n_x
    at = lax.broadcasted_iota(jnp.int32, (batch, batch), 0)
    block = at // slots
    step = (block % n_x) * n_r + block // n_x
    slot = (lax.axis_index(GROUP) ^ step) * slots + at % slots
    return (slot == placement).astype(F32).astype(BF16)


def head_kernel(out_ref):
    out_ref[...] = jnp.zeros_like(out_ref)


def stream_kernel(n_t, *refs):
    parts, (x_ref, squares_ref) = refs[:n_t], refs[n_t:]
    rows = parts[0].shape[0]
    t = lax.axis_index("tensor")
    for d in range(n_t):
        at = pl.multiple_of((t ^ d) * rows, rows)
        part = parts[d][...].astype(F32)
        x_ref[pl.ds(at, rows), :] = part
        squares = jnp.sum(part * part, axis=1, keepdims=True)
        squares_ref[pl.ds(at, rows), :] = jnp.broadcast_to(squares, (rows, LANES))


def first_kernel(n_g, n_x, slots, features, products, *refs):
    x_ref, squares, (placement_ref, gain_ref, w_ref) = refs[0], refs[1 : n_g + 1], refs[n_g + 1 : n_g + 4]
    normed_ref, rest_ref, own_ref, *sends, sem = refs[n_g + 4 :]
    move = pltpu.make_async_copy(w_ref.at[pl.ds(products, 3 - products)], rest_ref, sem)
    move.start()
    total = squares[0][...]
    for ref in squares[1:]:
        total = total + ref[...]
    scale = lax.rsqrt(total[:, :1] / features + EPS)
    normed = (x_ref[...] * scale * gain_ref[...]).astype(BF16)
    onehot = slot_onehot(placement_ref[...], slots, n_x)
    normed = jnp.dot(onehot, normed, preferred_element_type=F32).astype(BF16)
    normed_ref[...] = normed
    width = w_ref.shape[2]
    for j in range(products):
        for c in chunks(width):
            out = jnp.dot(normed, w_ref[j, :, c], preferred_element_type=F32)
            deliver(out, slice(j * width + c.start, j * width + c.stop), own_ref, sends)
    move.wait()


def collect(width, n_x, counts, refs):
    products, rest = [], []
    for i, count in enumerate(counts):
        own_ref, *received = refs[i * n_x : (i + 1) * n_x]
        total = own_ref[...]
        for ref in received:
            total = total + ref[...].astype(F32)
        products += [total[:, j * width : (j + 1) * width] for j in range(count)]
        rest.append(total[:, count * width :])
    return products, rest


def attend_kernel(n_x, counts, *refs):
    n = n_x * len(counts)
    lengths_ref, keys_ref, values_ref, out_ref = refs[n:]
    slots, width = out_ref.shape
    columns = keys_ref.shape[0]
    positions = columns // slots
    query, fresh_key, fresh_value = [
        p.astype(BF16).astype(F32) for p in collect(width, n_x, counts, refs[:n])[0]
    ]
    scale = 1.0 / math.sqrt(HEAD_DIM)
    column = lax.broadcasted_iota(jnp.int32, (slots, columns), 1)
    slot = lax.broadcasted_iota(jnp.int32, (slots, columns), 0)
    length = jnp.zeros((slots, columns), jnp.int32)
    for s in range(slots):
        length = jnp.where(slot == s, lengths_ref[s], length)
    live = (column >= slot * positions) & (column < slot * positions + length)
    heads = [slice(h, h + HEAD_DIM) for h in range(0, width, HEAD_DIM)]
    scores = [
        scale
        * lax.dot_general(
            query[:, h].astype(BF16), keys_ref[:, h], (((1,), (1,)), ((), ())), preferred_element_type=F32
        )
        for h in heads
    ]
    own_scores = [scale * jnp.sum(query[:, h] * fresh_key[:, h], axis=1, keepdims=True) for h in heads]
    for h, score, own_score in zip(heads, scores, own_scores):
        top = jnp.maximum(jnp.max(jnp.where(live, score, -jnp.inf), axis=1, keepdims=True), own_score)
        probs = jnp.where(live, jnp.exp(score - top), 0.0)
        self_prob = jnp.exp(own_score - top)
        total = jnp.sum(probs, axis=1, keepdims=True) + self_prob
        weights = (probs / total).astype(BF16)
        self_weight = (self_prob / total).astype(BF16).astype(F32)
        out = jnp.dot(weights, values_ref[:, h], preferred_element_type=F32)
        out_ref[:, h] = (out + self_weight * fresh_value[:, h]).astype(BF16)


def out_kernel(n_g, n_x, starts, *refs):
    parts, (placement_ref, w_ref) = refs[:n_g], refs[n_g : n_g + 2]
    owns, sends = refs[n_g + 2 :: 2], refs[n_g + 3 :: 2]
    gathered = jnp.concatenate([p[...].astype(F32) for p in parts], axis=0).astype(BF16)
    onehot = slot_onehot(placement_ref[...], parts[0].shape[0], n_x)
    rows = lax.dot_general(
        onehot, gathered, (((0,), (0,)), ((), ())), preferred_element_type=F32
    ).astype(BF16)
    for own_ref, send_ref, start in zip(owns, sends, starts):
        for c in chunks(own_ref.shape[1]):
            out = jnp.dot(
                rows, w_ref[:, start + c.start : start + c.stop], preferred_element_type=F32
            )
            own_ref[:, c] = out
            send_ref[:, c] = out.astype(BF16)


def join(steps, block, start, x_ref, terms_ref, received, gain_ref, attended_ref, scratch):
    rows, width = attended_ref.shape
    columns = slice(start, start + width)
    total = terms_ref[...]
    for ref in received:
        total = total + ref[...].astype(F32)
    scratch[...] = (x_ref[:, columns] + total).astype(BF16).astype(F32)
    at = pl.multiple_of(lax.axis_index("tensor") * rows, rows)
    attended_ref[...] = scratch[pl.ds(at, rows), :].astype(BF16)
    g = lax.axis_index(GROUP)
    xp = jnp.concatenate(
        [scratch[pl.ds(pl.multiple_of((g ^ e) * block, block), block), :] for e in steps], axis=0
    )
    return jnp.sum(xp * xp, axis=1, keepdims=True), (xp * gain_ref[:, columns]).astype(BF16)


def piece_kernel(steps, block, start, *refs):
    x_ref, terms_ref, received, gain_ref, w_ref = refs[:5]
    before, (attended_ref, sums_ref, squares_ref, scratch) = refs[5:-4], refs[-4:]
    squares, gained = join(
        steps, block, start, x_ref, terms_ref, [received], gain_ref, attended_ref, scratch
    )
    squares_ref[...] = (before[1][...] if before else 0.0) + jnp.broadcast_to(squares, squares_ref.shape)
    width = w_ref.shape[2]
    for j in range(3):
        for c in chunks(width):
            at = slice(j * width + c.start, j * width + c.stop)
            out = jnp.dot(
                gained, w_ref[j, start : start + gained.shape[1], c], preferred_element_type=F32
            )
            sums_ref[:, at] = out + before[0][:, at] if before else out


def last_kernel(steps, block, start, outs, *refs):
    x_ref, terms_ref, received, gain_ref, w_ref = refs[:5]
    before, (attended_ref, gained_ref, *kept, scratch) = refs[5 : -outs - 3], refs[-outs - 3 :]
    squares, gained = join(
        steps, block, start, x_ref, terms_ref, [received], gain_ref, attended_ref, scratch
    )
    gained_ref[...] = gained
    if before:
        squares = squares + before[1][:, :1]
    products, _, width = w_ref.shape
    deliver(tail_of(squares), slice(products * width, products * width + LANES), kept[0], kept[1:])
    for j in range(products):
        for c in chunks(width):
            at = slice(j * width + c.start, j * width + c.stop)
            out = jnp.dot(gained, w_ref[j, :, c], preferred_element_type=F32)
            deliver(out + before[0][:, at] if before else out, at, kept[0], kept[1:])


def rest_kernel(start, products, outs, *refs):
    gained_ref, weights = refs[0], refs[1 : 1 + products]
    before, kept = refs[1 + products : -outs], refs[-outs:]
    gained = gained_ref[...]
    for j, w_ref in enumerate(weights):
        width = w_ref.shape[2]
        for c in chunks(width):
            out = jnp.dot(gained, w_ref[0, :, c], preferred_element_type=F32)
            if before:
                at = (start + j) * width
                out = out + before[0][:, at + c.start : at + c.stop]
            deliver(out, slice(j * width + c.start, j * width + c.stop), kept[0], kept[1:])


def mixer_kernel(n_x, features, counts, *refs):
    n = n_x * len(counts)
    outer_taps, outer_state, inner_taps, inner_state, out_ref = refs[n:]
    products, rest = collect(out_ref.shape[1], n_x, counts, refs[:n])
    scale = lax.rsqrt(jnp.sum(rest[0], axis=1, keepdims=True) / features + EPS)
    branches = [p * scale for p in products]
    conv = [
        outer_taps[0, j : j + 1] * branches[j]
        + outer_taps[1, j : j + 1] * outer_state[0, j].astype(F32)
        + outer_taps[2, j : j + 1] * outer_state[1, j].astype(F32)
        for j in range(3)
    ]
    filtered = (
        inner_taps[0:1] * (conv[0] * conv[2])
        + inner_taps[1:2] * inner_state[0].astype(F32)
        + inner_taps[2:3] * inner_state[1].astype(F32)
    )
    out_ref[...] = (conv[1] * filtered).astype(BF16)


def local(
    n_t,
    n_x,
    n_r,
    residual,
    attn_gain,
    attn_proj,
    cache_keys,
    cache_values,
    lengths,
    placement,
    out_proj,
    mix_gain,
    mix_proj,
    outer_taps,
    outer_state,
    inner_taps,
    inner_state,
):
    n_g = n_x * n_r
    rows, depth = residual.shape
    slots = lengths.shape[0]
    batch = placement.shape[0]
    width = attn_proj.shape[2]
    features = depth * n_g
    placement = placement.reshape(1, batch)
    attn_gain, mix_gain = attn_gain.reshape(1, depth), mix_gain.reshape(1, depth)

    def swap(x, axes, n):
        return [lax.ppermute(x[d - 1], axes, [(i, i ^ d) for i in range(n)]) for d in range(1, n)]

    steps = [d * n_r + a for a in range(n_r) for d in range(n_x)]

    def blocks(products, tail):
        return [shape((n_x * slots, products * width + tail), F32)] * n_r

    def spread(kept, dtype=BF16):
        for a in range(1, n_r):
            received = lax.ppermute(kept[a], "role", [(i, i ^ a) for i in range(n_r)])
            kept[0] = kept[0] + received
        parts = [kept[0][d * slots : (d + 1) * slots] for d in range(n_x)]
        arrived = parts[:1]
        for d in range(1, n_x):
            arrived.append(lax.ppermute(parts[d].astype(dtype), "rows", [(i, i ^ d) for i in range(n_x)]))
        return arrived

    def cost(k, n):
        return dict(flops=2 * batch * k * n, moved=2 * k * n)

    (head,) = call(head_kernel, [shape((8, LANES), F32)], [], limit=2, flops=attn_proj.size * 64 * 40, moved=attn_proj.size * 80)()
    residual, head = lax.optimization_barrier((residual, head))
    parts = [residual] + swap([residual] * n_t, "tensor", n_t)
    small = max(LANES, depth * SHARE // 8 // LANES * LANES)
    sizes, starts = [small, depth - small], [0, small]
    last = PIECES - 1

    def last_piece(start, products):
        window = (slice(start, start + products), slice(starts[last], depth), slice(None))
        return mix_proj, window, (products, sizes[last], width)

    later = [last_piece(j, 1) for j in range(3)]
    attn_w = pltpu.with_memory_space_constraint(attn_proj, pltpu.VMEM)
    count = FIRST_SPLIT[0]
    rest = 3 - count
    keys, values = [c.reshape(-1, width) for c in (cache_keys, cache_values)]
    x, squares = call(
        functools.partial(stream_kernel, n_t),
        [shape((batch, depth), F32), shape((batch, LANES), F32)],
        [VMEM] * n_t,
        limit=2,
        ordered=[head],
    )(*parts)
    squares = [squares] + swap([squares] * n_g, GROUP, n_g)
    normed, rest_w, *kept, keys, values, first_mid = call(
        functools.partial(first_kernel, n_g, n_x, slots, features, count),
        [shape((batch, depth), BF16), pltpu.VMEM((rest, depth, width), BF16)] + blocks(count, 0),
        [VMEM] * (n_g + 4),
        scratch=[pltpu.SemaphoreType.DMA],
        **cost(depth, count * width),
        loads=[whole(keys), whole(values), later[1]],
    )(x, *squares, placement, attn_gain, attn_w)
    mid = [first_mid]
    arrived = spread(kept, F32)
    kept = call(
        functools.partial(rest_kernel, 0, rest, n_r),
        blocks(rest, 0),
        [VMEM] * 2,
        **cost(depth, rest * width),
    )(normed, rest_w)
    arrived += spread(list(kept))
    own = kept[0]
    out_w = pltpu.with_memory_space_constraint(out_proj, pltpu.VMEM)

    mid += load(later[2:], own)
    (slot_out,) = call(
        functools.partial(attend_kernel, n_x, FIRST_SPLIT),
        [shape((slots, width), BF16)],
        [VMEM] * len(arrived) + [SMEM, VMEM, VMEM],
        flops=mix_proj.size * 64 * 40,
        moved=cache_keys.size * 4,
        ordered=mid,
    )(*arrived, lengths, keys, values)

    gathered = [slot_out] + swap([slot_out] * n_g, GROUP, n_g)
    gathered = [gathered[e] for e in steps]
    terms = call(
        functools.partial(out_kernel, n_g, n_x, starts),
        [shape((batch, n), t) for n in sizes for t in (F32, BF16)],
        [VMEM] * (n_g + 2),
    )(*gathered, placement, out_w)

    (first_w,) = load(later[:1], terms[0])

    totals, sends = list(terms[::2]), list(terms[1::2])
    strides = [1 << i for i in range(n_t.bit_length() - 1)]
    for i in range(len(strides)):
        if i:
            totals = [a + b.astype(F32) for a, b in zip(totals, received)]
            sends = [a.astype(BF16) for a in totals]
        received = []
        for p, send in enumerate(sends):
            stride = strides[i] if p % 2 == 0 else strides[-1 - i]
            received.append(lax.ppermute(send, "tensor", [(k, k ^ stride) for k in range(n_t)]))

    mix_w = pltpu.with_memory_space_constraint(mix_proj, pltpu.VMEM)
    attended, before = [], []
    for p in range(last):
        out, *before = call(
            functools.partial(piece_kernel, steps, slots, starts[p]),
            [shape((rows, sizes[p]), BF16), shape((batch, 3 * width), F32), shape((batch, LANES), F32)],
            [VMEM] * (5 + len(before)),
            scratch=[pltpu.VMEM((batch, sizes[p]), F32)],
            **cost(sizes[p], 3 * width),
        )(x, totals[p], received[p], mix_gain, mix_w, *before)
        attended.append(out)

    count = SECOND_SPLIT[0]
    out, gained, *kept = call(
        functools.partial(last_kernel, steps, slots, starts[last], n_r),
        [shape((rows, sizes[last]), BF16), shape((batch, sizes[last]), BF16)]
        + blocks(count, LANES),
        [VMEM] * (5 + len(before)),
        scratch=[pltpu.VMEM((batch, sizes[last]), F32)],
        **cost(sizes[last], count * width),
    )(x, totals[-1], received[-1], mix_gain, first_w, *before)
    attended.append(out)
    arrived = spread(kept)
    rest = 3 - count
    kept = call(
        functools.partial(rest_kernel, count, rest, n_r),
        blocks(rest, 0),
        [VMEM] * (1 + rest + len(before[:1])),
        **cost(sizes[last], rest * width),
    )(gained, *mid, *before[:1])
    arrived += spread(list(kept))
    (gated,) = call(
        functools.partial(mixer_kernel, n_x, features, SECOND_SPLIT),
        [shape((slots, width), BF16)],
        [VMEM] * (len(arrived) + 4),
        flops=slots * width * 40,
        moved=slots * width * 40,
    )(*arrived, outer_taps, outer_state, inner_taps, inner_state)
    return (jnp.concatenate(attended, axis=1), gated)


def solution(mesh):
    n_t = mesh.shape["tensor"]
    n_x, n_r = mesh.shape["rows"], mesh.shape["role"]
    for n in (n_t, n_x, n_r):
        assert n & (n - 1) == 0, "axis size"

    def body(*args):
        return local(n_t, n_x, n_r, *args)

    return jax.shard_map(
        body,
        mesh=mesh,
        in_specs=(
            P(("groups", "tensor"), ("rows", "role")),
            P(("rows", "role")),
            P(None, ("rows", "role"), "tensor"),
            P(("groups", "rows", "role"), None, "tensor"),
            P(("groups", "rows", "role"), None, "tensor"),
            P(("groups", "rows", "role")),
            P("groups"),
            P("tensor", ("rows", "role")),
            P(("rows", "role")),
            P(None, ("rows", "role"), "tensor"),
            P(None, None, "tensor"),
            P(None, None, ("groups", "rows", "role"), "tensor"),
            P(None, "tensor"),
            P(None, ("groups", "rows", "role"), "tensor"),
        ),
        out_specs=(
            P(("groups", "tensor"), ("rows", "role")),
            P(("groups", "rows", "role"), "tensor"),
        ),
        check_vma=False,
    )
```
